256 devices in a mesh: row: 16 (over x, z_lo, core), col: 16 (over y, z_hi).
Axes of the slice: x: 4, y: 4, z: 8 (z_hi: 4, z_lo: 2; z = z_hi * 2 + z_lo), core: 2. Of those that a mesh axis runs over, the one named last changes fastest.
Arguments:
- object_field: float32 [2, 2, 6144, 6144], P(None, None, 'row', 'col'), may hold values from -4 to 4
- probe_wave: float32 [2, 256, 256], replicated, may hold values from -4 to 4
- prop_phase: float32 [256, 256], replicated, may hold values from -3.140625 to 3.140625
- corners: int32 [16, 16, 2, 2], P('row', 'col'), may hold values from 0 to 383
- counts: int32 [16, 16], P('row', 'col'), may hold values from 1 to 2, as said below
- intensities: float32 [16, 16, 2, 256, 256], P('row', 'col'), may hold values from 0 to 2
Outputs:
- updated_object: float32 [2, 2, 6144, 6144], P(None, None, 'row', 'col')
The draws below stay inside these ranges and needn't reach their ends.
Inputs may be any that keep to these rules, and one draw needn't show every extreme that they name: Slots from counts[a, b] on are empty; in every draw some device has all 2 slots live.
All inputs are finite; a program needn't handle non-finite values.
Results may differ from the reference program's by a relative error of at most 0.0003.
Values sent between devices are 32-bit elements; how exact they have to be, the bound alone decides.
No kernel may reach another device: no remote copies, remote signals or barrier semaphores. Data moves between devices by JAX's collectives and lax.ppermute only.
A program may use at most 64 MiB of HBM per device.

```python
import jax
import jax.numpy as jnp
from jax import lax

WIN = 256
TILE = 384
SLOTS = 2
STEPS = 2
GRID_R = 16
GRID_C = 16
HEIGHT = 6144
WIDTH = 6144


def draw_counts(key, part):
    first_key, second_key, third_key = jax.random.split(jax.random.fold_in(key, 11), 3)
    grid_shape = (GRID_R, GRID_C)
    left_factor = jax.random.randint(first_key, grid_shape, 0, SLOTS)
    right_factor = jax.random.randint(second_key, grid_shape, 0, SLOTS)
    drawn = 1 + left_factor * right_factor // (SLOTS - 1)
    chosen = jax.random.randint(third_key, (), 0, GRID_R * GRID_C)
    flat_counts = drawn.reshape(-1)
    flat_counts = jnp.where(lax.iota(jnp.int32, GRID_R * GRID_C) == chosen, SLOTS, flat_counts)
    return flat_counts.reshape(grid_shape).astype(jnp.int32)


def set_ends(values, key, smallest, high):
    spot = [jax.random.randint(jax.random.fold_in(key, axis), (), 0, length) for axis, length in enumerate(values.shape)]
    longest = values.shape.index(max(values.shape))
    beside = spot[:longest] + [(spot[longest] + 1) % values.shape[longest]] + spot[longest + 1:]
    return values.at[tuple(spot)].set(smallest).at[tuple(beside)].set(high)


def block_levels(own_key, extent, cuts, low, largest):
    level, own = 1.0, jax.random.fold_in(own_key, 6)
    for position, blocks in cuts:
        heights = jnp.exp(jax.random.uniform(jax.random.fold_in(own, position), (blocks,), jnp.float32, low / len(cuts), largest / len(cuts)))
        level = level * jnp.repeat(heights, extent[position] // blocks).reshape([-1 if axis == position else 1 for axis in range(len(extent))])
    return level


def scatter_about(own_key, shape, spread, limit, pieces=(), kind=jnp.bfloat16):
    loudness = block_levels(own_key, shape, pieces, -0.22, 0.18) if pieces else 1.0
    values = jax.random.normal(own_key, shape, jnp.float32) * spread * loudness
    return jnp.minimum(jnp.maximum(values, -limit), limit).astype(kind)


def setup_inputs(seed: int = 0) -> dict:
    arg_keys = jax.random.split(jax.random.key(seed), 7)
    return {
        "object_field": scatter_about(arg_keys[0], (2, 2, HEIGHT, WIDTH), 0.7, 4.0, ((2, 16), (3, 16)), jnp.float32),
        "probe_wave": scatter_about(arg_keys[1], (2, WIN, WIN), 0.7, 4.0, (), jnp.float32),
        "prop_phase": jnp.clip(jax.random.uniform(arg_keys[2], (WIN, WIN), jnp.float32, -3.140625, 3.140625), -3.140625, 3.140625),
        "corners": set_ends(jax.random.randint(arg_keys[3], (GRID_R, GRID_C, SLOTS, 2), 0, TILE), jax.random.fold_in(arg_keys[3], 1), 0, TILE - 1).astype(jnp.int32),
        "counts": draw_counts(jax.random.fold_in(arg_keys[6], 71), 0),
        "intensities": jnp.clip(2.0 * jax.random.uniform(arg_keys[5], (GRID_R, GRID_C, SLOTS, WIN, WIN), jnp.float32) ** block_levels(arg_keys[5], (GRID_R, GRID_C, SLOTS, WIN, WIN), ((0, 16), (1, 16)), -0.2, 0.2), 0.0, 2.0),
    }


update_rate = 0.1


def complex_times(left_pair, right_pair):
    return (left_pair[0] * right_pair[0] - left_pair[1] * right_pair[1],
            left_pair[0] * right_pair[1] + left_pair[1] * right_pair[0])


def conj_times(left_pair, right_pair):
    return (left_pair[0] * right_pair[0] + left_pair[1] * right_pair[1],
            left_pair[0] * right_pair[1] - left_pair[1] * right_pair[0])


def spectrum(field_pair, inverse):
    joined = lax.complex(field_pair[0], field_pair[1])
    if inverse:
        result = jnp.fft.ifft2(joined, norm="ortho")
    else:
        result = jnp.fft.fft2(joined, norm="ortho")
    return (jnp.real(result), jnp.imag(result))


def window_grads(window_block, probe_pair, phase_pair, measured, live_flag):
    slice_one = (window_block[0, 0], window_block[0, 1])
    slice_two = (window_block[1, 0], window_block[1, 1])
    psi_one = complex_times(probe_pair, slice_one)
    psi_two = spectrum(complex_times(phase_pair, spectrum(psi_one, False)), True)
    far_field = spectrum(complex_times(psi_two, slice_two), False)
    misfit = live_flag * (far_field[0] * far_field[0] + far_field[1] * far_field[1] - measured)
    exit_grad = spectrum((misfit * far_field[0], misfit * far_field[1]), True)
    grad_two = conj_times(psi_two, exit_grad)
    back_grad = spectrum(conj_times(phase_pair, spectrum(conj_times(slice_two, exit_grad), False)), True)
    grad_one = conj_times(probe_pair, back_grad)
    return jnp.stack([jnp.stack(grad_one), jnp.stack(grad_two)])


def reference(object_field, probe_wave, prop_phase, corners, counts, intensities):
    phase_pair = (jnp.cos(prop_phase), jnp.sin(prop_phase))
    probe_pair = (probe_wave[0], probe_wave[1])
    current = object_field
    zero_index = jnp.zeros((), jnp.int32)
    for sweep_index in range(STEPS):
        padded = jnp.concatenate([current, current[:, :, :WIN, :]], 2)
        padded = jnp.concatenate([padded, padded[:, :, :, :WIN]], 3)

        def visit_device(totals, device):
            tile_row = device // GRID_C
            tile_col = device % GRID_C
            for slot_index in range(SLOTS):
                start_row = (tile_row * TILE + corners[tile_row, tile_col, slot_index, 0]).astype(jnp.int32)
                start_col = (tile_col * TILE + corners[tile_row, tile_col, slot_index, 1]).astype(jnp.int32)
                start_at = (zero_index, zero_index, start_row, start_col)
                window_block = lax.dynamic_slice(padded, start_at, (2, 2, WIN, WIN))
                live_flag = (slot_index < counts[tile_row, tile_col]).astype(current.dtype)
                measured = intensities[tile_row, tile_col, slot_index]
                window_grad = window_grads(window_block, probe_pair, phase_pair, measured, live_flag)
                previous = lax.dynamic_slice(totals, start_at, (2, 2, WIN, WIN))
                totals = lax.dynamic_update_slice(totals, previous + window_grad, start_at)
            return totals, None

        totals = jnp.zeros(padded.shape, current.dtype)
        totals, unused = lax.scan(visit_device, totals, jnp.arange(GRID_R * GRID_C, dtype=jnp.int32))
        folded = totals[:, :, :HEIGHT, :WIDTH]
        folded = folded.at[:, :, :WIN, :].add(totals[:, :, HEIGHT:, :WIDTH])
        folded = folded.at[:, :, :, :WIN].add(totals[:, :, :HEIGHT, WIDTH:])
        folded = folded.at[:, :, :WIN, :WIN].add(totals[:, :, HEIGHT:, WIDTH:])
        current = current - update_rate * folded
    return current
```

```python
import math

import jax
import jax.numpy as jnp
from jax import lax
from jax.experimental import pallas as pl
from jax.experimental.pallas import tpu as pltpu
from jax.sharding import PartitionSpec as P


STEPS = 2
RATE = 0.1
WIN = 256
TILE = 384
BLK = 128
SLOTS = 2
f32 = jnp.float32
bf16 = jnp.bfloat16

ROWS = {"a": (0, 256), "b": (256, 384), "c": (384, 640)}
COLS = {"l": (0, 256), "m": (256, 384), "r": (384, 640)}
NAMES = [i + j for i in "abc" for j in "lmr"]


def piece_shape(name):
    r, c = ROWS[name[0]], COLS[name[1]]
    return (2, r[1] - r[0], c[1] - c[0])


def locate(q, p):
    row = "aabcc"[q]
    col = "llmrr"[p]
    return row + col, q * BLK - ROWS[row][0], p * BLK - COLS[col][0]


def shifted(block, axis, distance):
    n = lax.axis_size(axis)
    return lax.ppermute(block, axis, [((i - distance) % n, i) for i in range(n)])


def split(x):
    hi = x.astype(bf16)
    return hi, (x - hi.astype(f32)).astype(bf16)


def mm(a, b):
    return lax.dot_general(a, b, (((1,), (0,)), ((), ())), preferred_element_type=f32)


def mm_right(x, tab):
    hi, lo = split(x)
    return mm(jnp.concatenate([hi, hi, lo], 1), tab)


def mm_left(tab, x):
    hi, lo = split(x)
    return mm(tab, jnp.concatenate([hi, lo, hi], 0))


def fft2(re, im, right, left):
    k1 = mm_right(re + im, right[0])
    k2 = mm_right(re, right[1])
    k3 = mm_right(im, right[2])
    re, im = k1 - k3, k1 + k2
    k1 = mm_left(left[0], re + im)
    k2 = mm_left(left[1], re)
    k3 = mm_left(left[2], im)
    return k1 - k3, k1 + k2


def ifft2(re, im, right, left):
    out_im, out_re = fft2(im, re, right, left)
    return out_re, out_im


def times(a, b):
    return a[0] * b[0] - a[1] * b[1], a[0] * b[1] + a[1] * b[0]


def conj_times(a, b):
    return a[0] * b[0] + a[1] * b[1], a[0] * b[1] - a[1] * b[0]


def masks(info, slot, dim):
    corner = info[2 * slot + dim]
    index = lax.broadcasted_iota(jnp.int32, (BLK, BLK), dim)
    out = []
    for q in range(5):
        pixel = index + q * BLK
        out.append((pixel >= corner) & (pixel < corner + WIN))
    return out


def read_window(info, pieces, slot, dst):
    rows, cols = masks(info, slot, 0), masks(info, slot, 1)
    for comp in range(2):
        for h in range(2):
            for g in range(2):
                value = None
                for q in range(h, 5, 2):
                    line = None
                    for p in range(g, 5, 2):
                        name, i, j = locate(q, p)
                        block = pieces[name][comp, i:i + BLK, j:j + BLK]
                        line = block if line is None else jnp.where(cols[p], block, line)
                    value = line if value is None else jnp.where(rows[q], line, value)
                dst[comp, slot * WIN + h * BLK:slot * WIN + (h + 1) * BLK, g * BLK:(g + 1) * BLK] = value


def write_grads(info, grads, outs):
    picks = [(masks(info, slot, 0), masks(info, slot, 1)) for slot in range(SLOTS)]
    for q in range(5):
        for p in range(5):
            name, i, j = locate(q, p)
            if name[0] == "c":
                name, j = "c", p * BLK
            for comp in range(2):
                total = None
                for slot in range(SLOTS):
                    rows, cols = picks[slot]
                    r0, c0 = slot * WIN + (q % 2) * BLK, (p % 2) * BLK
                    part = jnp.where(rows[q] & cols[p], grads[comp, r0:r0 + BLK, c0:c0 + BLK], 0.0)
                    total = part if total is None else total + part
                outs[name][comp, i:i + BLK, j:j + BLK] = total * RATE


GRAD_NAMES = ["al", "am", "ar", "bl", "bm", "br", "c"]


def grad_shape(name):
    return (2, 256, 640) if name == "c" else piece_shape(name)


def setup_kernel(info, probe, cosine, sine, rolled, right, left):
    for slot in range(SLOTS):
        for comp in range(2):
            turned = pltpu.roll(probe[comp], lax.rem(info[2 * slot], WIN), 0)
            rolled[comp, slot * WIN:(slot + 1) * WIN, :] = pltpu.roll(turned, lax.rem(info[2 * slot + 1], WIN), 1)
    for t, table in enumerate([cosine[...], -(cosine[...] + sine[...]), cosine[...] - sine[...]]):
        hi, lo = split(table)
        right[t, 0:WIN] = hi
        right[t, WIN:2 * WIN] = lo
        right[t, 2 * WIN:] = hi
        left[t, :, 0:WIN] = hi
        left[t, :, WIN:2 * WIN] = hi
        left[t, :, 2 * WIN:] = lo


def slot_rows(slot):
    return slice(slot * WIN, (slot + 1) * WIN)


def psi_kernel(info, probe, prop, right, left, *refs):
    pieces = dict(zip(NAMES, refs[:9]))
    psi, window = refs[9], refs[10]
    h = (prop[0], prop[1])
    for slot in range(SLOTS):
        rows = slot_rows(slot)
        read_window(info, pieces, slot, window)
        field = times((probe[0, rows], probe[1, rows]), (window[0, rows], window[1, rows]))
        field = ifft2(*times(h, fft2(*field, right, left)), right, left)
        psi[0, rows], psi[1, rows] = field


def exit_kernel(info, psi, measured, right, left, *refs):
    pieces = dict(zip(NAMES, refs[:9]))
    outs = dict(zip(GRAD_NAMES, refs[9:16]))
    back, window, grads = refs[16], refs[17], refs[18]
    for slot in range(SLOTS):
        rows = slot_rows(slot)
        live = (slot < info[4]).astype(f32)
        read_window(info, pieces, slot, window)
        wave = (psi[0, rows], psi[1, rows])
        far = fft2(*times(wave, (window[0, rows], window[1, rows])), right, left)
        misfit = live * (far[0] * far[0] + far[1] * far[1] - measured[rows])
        leave = ifft2(misfit * far[0], misfit * far[1], right, left)
        grads[0, rows], grads[1, rows] = conj_times((psi[0, rows], psi[1, rows]), leave)
        back[0, rows], back[1, rows] = conj_times((window[0, rows], window[1, rows]), leave)
    write_grads(info, grads, outs)


def back_kernel(info, probe, prop, back, right, left, *refs):
    outs = dict(zip(GRAD_NAMES, refs[:7]))
    grads = refs[7]
    h = (prop[0], prop[1])
    for slot in range(SLOTS):
        rows = slot_rows(slot)
        field = fft2(back[0, rows], back[1, rows], right, left)
        field = ifft2(*conj_times(h, field), right, left)
        grads[0, rows], grads[1, rows] = conj_times((probe[0, rows], probe[1, rows]), field)
    write_grads(info, grads, outs)


smem = pl.BlockSpec(memory_space=pltpu.SMEM)
vmem = pl.BlockSpec(memory_space=pltpu.VMEM)
stacked = (2, SLOTS * WIN, WIN)
scratch = pltpu.VMEM(stacked, f32)
INTERPRET = False


def call(kernel, name, shapes, n_inputs, scratches):
    return pl.pallas_call(
        kernel,
        name=name,
        out_shape=[jax.ShapeDtypeStruct(s, d) for s, d in shapes],
        in_specs=[smem] + [vmem] * (n_inputs - 1),
        out_specs=[vmem] * len(shapes),
        scratch_shapes=scratches,
        interpret=INTERPRET,
    )


def per_device(object_field, probe_wave, prop_phase, corners, counts, intensities):
    info = jnp.concatenate([corners.reshape(-1), counts.reshape(-1)])
    measured = intensities.reshape(SLOTS * WIN, WIN)
    grad_outs = [(grad_shape(n), f32) for n in GRAD_NAMES]

    now = []
    for s in range(2):
        tile = object_field[s]
        now.append({
            n: lax.slice(tile, (0, ROWS[n[0]][0], COLS[n[1]][0]), (2, ROWS[n[0]][1], COLS[n[1]][1]))
            for n in ("al", "am", "bl", "bm")
        })

    def fetch_cols(x):
        x["ar"] = shifted(x["al"], "col", -1)
        x["br"] = shifted(x["bl"], "col", -1)
        x["cl"] = shifted(x["al"], "row", -1)
        x["cm"] = shifted(x["am"], "row", -1)

    fetch_cols(now[0])
    now[0]["cr"] = shifted(now[0]["ar"], "row", -1)
    held = lax.optimization_barrier((now[0]["ar"], now[1]["al"], now[1]["am"], now[1]["bl"]))
    now[1]["al"], now[1]["am"], now[1]["bl"] = held[1:]
    fetch_cols(now[1])
    now[1]["cr"] = shifted(now[1]["ar"], "row", -1)

    index = lax.iota(jnp.int32, WIN)
    angles = (index[:, None] * index[None, :] % WIN).astype(f32) * (2.0 * math.pi / WIN)
    norm = 1.0 / math.sqrt(WIN)
    rolled, right, left = call(
        setup_kernel, "setup",
        [(stacked, f32), ((3, 3 * WIN, WIN), bf16), ((3, WIN, 3 * WIN), bf16)], 4, [],
    )(info, probe_wave, jnp.cos(angles) * norm, jnp.sin(angles) * norm)
    prop = jnp.stack([jnp.cos(prop_phase), jnp.sin(prop_phase)])

    for step in range(STEPS):
        last = step == STEPS - 1
        (psi,) = call(psi_kernel, "psi", [(stacked, f32)], 14, [scratch])(
            info, rolled, prop, right, left, *[now[0][n] for n in NAMES])
        *grads2, back = call(exit_kernel, "exit", grad_outs + [(stacked, f32)], 14, [scratch, scratch])(
            info, psi, measured, right, left, *[now[1][n] for n in NAMES])
        grads1 = call(back_kernel, "back", grad_outs, 6, [scratch])(info, rolled, prop, back, right, left)
        grads = [dict(zip(GRAD_NAMES, grads1)), dict(zip(GRAD_NAMES, grads2))]
        for s in (1, 0):
            x, g = now[s], grads[s]
            above = shifted(g["c"], "row", 1)
            left_b = shifted(g["br"], "col", 1)
            if not last:
                right_b = shifted(g["bl"], "col", -1)
            al = g["al"] + above[:, :, :256]
            ar = g["ar"] + above[:, :, 384:]
            left_a = shifted(ar, "col", 1)
            new = {
                "am": x["am"] - (g["am"] + above[:, :, 256:384]),
                "bm": x["bm"] - g["bm"],
                "al": x["al"] - (al + left_a),
                "bl": x["bl"] - (g["bl"] + left_b),
            }
            if not last:
                right_a = shifted(al, "col", -1)
                new["ar"] = x["ar"] - (ar + right_a)
                new["br"] = x["br"] - (g["br"] + right_b)
                for j in "mlr":
                    new["c" + j] = shifted(new["a" + j], "row", -1)
            now[s] = new
    return jnp.stack([
        jnp.concatenate([
            jnp.concatenate([x["al"], x["am"]], 2),
            jnp.concatenate([x["bl"], x["bm"]], 2),
        ], 1)
        for x in now
    ])


def solution(mesh):
    return jax.shard_map(
        per_device,
        mesh=mesh,
        in_specs=(
            P(None, None, "row", "col"),
            P(),
            P(),
            P("row", "col", None, None),
            P("row", "col"),
            P("row", "col", None, None, None),
        ),
        out_specs=P(None, None, "row", "col"),
        check_vma=False,
    )
```

```python
import math

import jax
import jax.numpy as jnp
from jax import lax
from jax.experimental import pallas as pl
from jax.experimental.pallas import tpu as pltpu
from jax.sharding import PartitionSpec as P


STEPS = 2
RATE = 0.1
WIN = 256
BLK = 128
SLOTS = 2
f32 = jnp.float32
bf16 = jnp.bfloat16

ROWS = {"a": (0, 256), "b": (256, 384)}
COLS = {"l": (0, 256), "m": (256, 384), "r": (384, 640)}
NAMES = ["al", "am", "ar", "bl", "bm", "br", "c"]
STACKED = (2, SLOTS * WIN, WIN)


def piece_shape(name):
    if name == "c":
        return STACKED
    r, c = ROWS[name[0]], COLS[name[1]]
    return (2, r[1] - r[0], c[1] - c[0])


def locate(q, p):
    row = "aab"[q]
    col = "llmrr"[p]
    return row + col, q * BLK - ROWS[row][0], p * BLK - COLS[col][0]


def shifted(block, axis, distance):
    n = lax.axis_size(axis)
    return lax.ppermute(block, axis, [((i - distance) % n, i) for i in range(n)])


def around(block, sign):
    rows, cols = lax.axis_size("row"), lax.axis_size("col")
    first, second = [], []
    for row in range(rows):
        for col in range(cols):
            x, z_lo, core = row // 4, row // 2 % 2, row % 2
            y, z_hi = col // 4, col % 4
            z = (2 * z_hi + z_lo - 3 * sign) % 8
            relay = (4 * x + 2 * (z % 2) + core) * cols + 4 * y + z // 2
            first.append((row * cols + col, relay))
            second.append((relay, row * cols + (col + sign) % cols))
    for route in (first, second):
        block = lax.ppermute(block, ("row", "col"), route)
    return block


def split(x):
    hi = x.astype(bf16)
    return hi, (x - hi.astype(f32)).astype(bf16)


def mm(a, b):
    return lax.dot_general(a, b, (((1,), (0,)), ((), ())), preferred_element_type=f32)


def mm_right(x, tab, t):
    hi, lo = split(x)
    return mm(hi, tab[t, 0]) + (mm(hi, tab[t, 1]) + mm(lo, tab[t, 0]))


def mm_left(tab, t, x):
    hi, lo = split(x)
    return mm(tab[t, 0], hi) + (mm(tab[t, 0], lo) + mm(tab[t, 1], hi))


def fft2(re, im, tab):
    k1 = mm_right(re + im, tab, 0)
    k2 = mm_right(re, tab, 1)
    k3 = mm_right(im, tab, 2)
    re, im = k1 - k3, k1 + k2
    k1 = mm_left(tab, 0, re + im)
    k2 = mm_left(tab, 1, re)
    k3 = mm_left(tab, 2, im)
    return k1 - k3, k1 + k2


def ifft2(re, im, tab):
    out_im, out_re = fft2(im, re, tab)
    return out_re, out_im


def times(a, b):
    return a[0] * b[0] - a[1] * b[1], a[0] * b[1] + a[1] * b[0]


def conj_times(a, b):
    return a[0] * b[0] + a[1] * b[1], a[0] * b[1] - a[1] * b[0]


def masks(info, slot, dim):
    corner = info[2 * slot + dim]
    index = lax.broadcasted_iota(jnp.int32, (BLK, BLK), dim)
    out = []
    for q in range(5):
        pixel = index + q * BLK
        out.append((pixel >= corner) & (pixel < corner + WIN))
    return out


def block_rows(slot, q):
    return pl.ds(pl.multiple_of(slot * WIN + (q - 3) * BLK, BLK), BLK)


def pick_columns(cols, pieces, comp, q, g):
    line = None
    for p in range(g, 5, 2):
        name, i, j = locate(q, p)
        block = pieces[name][comp, i:i + BLK, j:j + BLK]
        line = block if line is None else jnp.where(cols[p], block, line)
    return line


def read_window(info, pieces, slot, dst):
    rows, cols = masks(info, slot, 0), masks(info, slot, 1)

    @pl.loop(0, 2)
    def _(comp):
        for h in range(2):
            for g in range(2):
                value = None
                for q in range(h, 5, 2):
                    if q < 3:
                        line = pick_columns(cols, pieces, comp, q, g)
                    else:
                        line = pieces["c"][comp, block_rows(slot, q), g * BLK:(g + 1) * BLK]
                    value = line if value is None else jnp.where(rows[q], line, value)
                dst[comp, h * BLK:(h + 1) * BLK, g * BLK:(g + 1) * BLK] = value


def write_grads(info, grads, outs):
    picks = [(masks(info, slot, 0), masks(info, slot, 1)) for slot in range(SLOTS)]

    @pl.loop(0, 2)
    def _(comp):
        for q in range(3):
            for p in range(5):
                name, i, j = locate(q, p)
                total = None
                for slot in range(SLOTS):
                    rows, cols = picks[slot]
                    r0, c0 = slot * WIN + (q % 2) * BLK, (p % 2) * BLK
                    part = jnp.where(rows[q] & cols[p], grads[comp, r0:r0 + BLK, c0:c0 + BLK], 0.0)
                    total = part if total is None else total + part
                outs[name][comp, i:i + BLK, j:j + BLK] = total * RATE
        for slot in range(SLOTS):
            for q in (3, 4):
                for g in range(2):
                    r0, c0 = slot * WIN + (q % 2) * BLK, g * BLK
                    part = jnp.where(picks[slot][0][q], grads[comp, r0:r0 + BLK, c0:c0 + BLK], 0.0)
                    outs["c"][comp, block_rows(slot, q), c0:c0 + BLK] = part * RATE


def write_picked(above, pieces, picked):
    @pl.loop(0, SLOTS)
    def _(slot):
        cols = masks(above, slot, 1)

        @pl.loop(0, 2)
        def _(comp):
            for q in range(2):
                for g in range(2):
                    picked[comp, block_rows(slot, q + 3), g * BLK:(g + 1) * BLK] = pick_columns(cols, pieces, comp, q, g)


def pick_kernel(above, al, am, ar, picked):
    write_picked(above, {"al": al, "am": am, "ar": ar}, picked)


def sum_kernel(above, below, al, am, ar, *outs):
    grads, outs = {"al": al, "am": am, "ar": ar}, dict(zip(("al", "am", "ar"), outs))
    cols = [masks(above, slot, 1) for slot in range(SLOTS)]

    @pl.loop(0, 4)
    def _(index):
        comp, q = index // 2, index % 2
        rows = pl.ds(pl.multiple_of(q * BLK, BLK), BLK)
        for p in range(5):
            name, _, j = locate(0, p)
            total = grads[name][comp, rows, j:j + BLK]
            for slot in range(SLOTS):
                part = below[comp, block_rows(slot, q + 3), (p % 2) * BLK:(p % 2 + 1) * BLK]
                total = total + jnp.where(cols[slot][p], part, 0.0)
            outs[name][comp, rows, j:j + BLK] = total


def step_kernel(above, al, am, ar, gal, gam, gar, from_left, from_right, *outs):
    new = dict(zip(("al", "am", "ar"), outs))
    new["al"][...] = al[...] - (gal[...] + from_left[...])
    new["am"][...] = am[...] - gam[...]
    new["ar"][...] = ar[:, :WIN] - (gar[...] + from_right[...])
    write_picked(above, new, outs[3])


def setup_kernel(info, probe, trig, rolled, tab):
    for slot in range(SLOTS):
        for comp in range(2):
            turned = pltpu.roll(probe[comp], lax.rem(info[2 * slot], WIN), 0)
            rolled[comp, slot * WIN:(slot + 1) * WIN, :] = pltpu.roll(turned, lax.rem(info[2 * slot + 1], WIN), 1)
    cosine, sine = trig[0] / math.sqrt(WIN), trig[1] / math.sqrt(WIN)
    for t, table in enumerate([cosine, -(cosine + sine), cosine - sine]):
        tab[t, 0], tab[t, 1] = split(table)


def slot_rows(slot):
    return pl.ds(pl.multiple_of(slot * WIN, WIN), WIN)


def psi_kernel(info, probe, trig, tab, *refs):
    pieces = dict(zip(NAMES, refs[:7]))
    psi, window = refs[7], refs[8]

    @pl.loop(0, SLOTS)
    def _(slot):
        rows = slot_rows(slot)
        read_window(info, pieces, slot, window)
        field = times((probe[0, rows], probe[1, rows]), (window[0], window[1]))
        field = times((trig[2], trig[3]), fft2(*field, tab))
        psi[0, rows], psi[1, rows] = ifft2(*field, tab)


def exit_kernel(info, psi, measured, tab, *refs):
    pieces = dict(zip(NAMES, refs[:7]))
    outs = dict(zip(NAMES, refs[7:14]))
    back, window, grads = refs[14], refs[15], refs[16]

    @pl.loop(0, SLOTS)
    def _(slot):
        rows = slot_rows(slot)
        live = (slot < info[4]).astype(f32)
        read_window(info, pieces, slot, window)
        far = fft2(*times((psi[0, rows], psi[1, rows]), (window[0], window[1])), tab)
        misfit = live * (far[0] * far[0] + far[1] * far[1] - measured[rows])
        leave = ifft2(misfit * far[0], misfit * far[1], tab)
        grads[0, rows], grads[1, rows] = conj_times((psi[0, rows], psi[1, rows]), leave)
        back[0, rows], back[1, rows] = conj_times((window[0], window[1]), leave)

    write_grads(info, grads, outs)


def back_kernel(info, probe, trig, back, tab, *refs):
    outs = dict(zip(NAMES, refs[:7]))
    grads = refs[7]

    @pl.loop(0, SLOTS)
    def _(slot):
        rows = slot_rows(slot)
        field = conj_times((trig[2], trig[3]), fft2(back[0, rows], back[1, rows], tab))
        field = ifft2(*field, tab)
        grads[0, rows], grads[1, rows] = conj_times((probe[0, rows], probe[1, rows]), field)

    write_grads(info, grads, outs)


smem = pl.BlockSpec(memory_space=pltpu.SMEM)
vmem = pl.BlockSpec(memory_space=pltpu.VMEM)
scratch = pltpu.VMEM(STACKED, f32)
window = pltpu.VMEM((2, WIN, WIN), f32)
INTERPRET = False


def call(kernel, shapes, scratches=()):
    def run(info, *rest):
        if not INTERPRET:
            rest = [pltpu.with_memory_space_constraint(x, pltpu.VMEM) for x in rest]
        return pl.pallas_call(
            kernel,
            out_shape=[pltpu.VMEM(s, d) for s, d in shapes],
            in_specs=[smem] + [vmem] * len(rest),
            out_specs=[vmem] * len(shapes),
            scratch_shapes=list(scratches),
            interpret=INTERPRET,
            compiler_params=pltpu.CompilerParams(vmem_limit_bytes=24 << 20),
        )(info, *rest)

    return run


def run(object_field, probe_wave, prop_phase, corners, counts, intensities):
    info = jnp.concatenate([corners.reshape(-1), counts.reshape(-1)])
    measured = intensities.reshape(SLOTS * WIN, WIN)
    field = (STACKED, f32)
    region = [(piece_shape(n), f32) for n in NAMES]
    top = ("al", "am", "ar")

    now = []
    for s in range(2):
        tile = object_field[s]
        now.append({
            n: lax.slice(tile, (0, ROWS[n[0]][0], COLS[n[1]][0]), (2, ROWS[n[0]][1], COLS[n[1]][1]))
            for n in ("al", "am", "bl", "bm")
        })
    part = now[0]["bl"].shape[1] // 2
    relayed = around(jnp.concatenate([now[0]["bl"][:, part:], now[1]["bl"]], 1), -1)
    now[1]["br"] = relayed[:, part:]
    above = shifted(corners.reshape(-1), "row", 1)
    for s, x in enumerate(now):
        source = x["al"] if s else object_field[0, :, :WIN + part, :WIN]
        x["ar"] = shifted(source, "col", -1)
        (picked,) = call(pick_kernel, [field])(above, *[x[n] for n in top])
        x["c"] = shifted(picked, "row", -1)

    now[0]["br"] = jnp.concatenate([now[0]["ar"][:, WIN:], relayed[:, :part]], 1)

    index = lax.iota(jnp.int32, WIN)
    product = index[:, None] * index[None, :] + jnp.array([WIN, 3 * WIN // 4], jnp.int32)[:, None, None]
    angles = (product % WIN).astype(f32) * (2.0 * math.pi / WIN)
    trig = jnp.cos(jnp.concatenate([angles, jnp.stack([prop_phase, prop_phase - math.pi / 2])]))
    rolled, tab = call(setup_kernel, [field, ((3, 2, WIN, WIN), bf16)])(info, probe_wave, trig)

    for step in range(STEPS):
        last = step == STEPS - 1
        (psi,) = call(psi_kernel, [field], [window])(
            info, rolled, trig, tab, *[now[0][n] for n in NAMES])
        *grads2, back = call(exit_kernel, region + [field], [window, scratch])(
            info, psi, measured, tab, *[now[1][n] for n in NAMES])
        grads1 = call(back_kernel, region, [scratch])(info, rolled, trig, back, tab)
        grads = [dict(zip(NAMES, grads1)), dict(zip(NAMES, grads2))]
        if last:
            relayed = around(jnp.concatenate([grads[0]["br"][:, part:], grads[1]["br"]], 1), 1)
            direct = shifted(grads[0]["br"][:, :part], "col", 1)
            left_b = [jnp.concatenate([direct, relayed[:, :part]], 1), relayed[:, part:]]
        for s in (1, 0):
            x, g = now[s], grads[s]
            found = shifted(g["c"], "row", 1)
            al, am, ar = call(sum_kernel, region[:3])(above, found, *[g[n] for n in top])
            left_a = shifted(ar, "col", 1)
            new = {"bm": x["bm"] - g["bm"]}
            if last:
                new["al"] = x["al"] - (al + left_a)
                new["am"] = x["am"] - am
                new["bl"] = x["bl"] - (g["bl"] + left_b[s])
            else:
                right_a = shifted(al, "col", -1)
                new["bl"] = x["bl"] - (g["bl"] + shifted(g["br"], "col", 1))
                new["br"] = x["br"] - (g["br"] + shifted(g["bl"], "col", -1))
                new["al"], new["am"], new["ar"], picked = call(step_kernel, region[:3] + [field])(
                    above, *[x[n] for n in top], al, am, ar, left_a, right_a)
                new["c"] = shifted(picked, "row", -1)
            now[s] = new
    return jnp.stack([
        jnp.concatenate([
            jnp.concatenate([x["al"], x["am"]], 2),
            jnp.concatenate([x["bl"], x["bm"]], 2),
        ], 1)
        for x in now
    ])


def solution(mesh):
    return jax.shard_map(
        run,
        mesh=mesh,
        in_specs=(
            P(None, None, "row", "col"),
            P(),
            P(),
            P("row", "col", None, None),
            P("row", "col"),
            P("row", "col", None, None, None),
        ),
        out_specs=P(None, None, "row", "col"),
        check_vma=False,
    )
```

```python
import math

import jax
import jax.numpy as jnp
from jax import lax
from jax.experimental import pallas as pl
from jax.experimental.pallas import tpu as pltpu
from jax.sharding import PartitionSpec as P


STEPS = 2
RATE = 0.1
WIN = 256
BLK = 128
SLOTS = 2
f32 = jnp.float32
bf16 = jnp.bfloat16

ROWS = {"a": (0, 256), "b": (256, 384)}
COLS = {"l": (0, 256), "m": (256, 384), "r": (384, 640)}
NAMES = ["al", "am", "ar", "bl", "bm", "br", "c"]
STACKED = (2, SLOTS * WIN, WIN)


def piece_shape(name):
    if name == "c":
        return STACKED
    r, c = ROWS[name[0]], COLS[name[1]]
    return (2, r[1] - r[0], c[1] - c[0])


def locate(q, p):
    row = "aab"[q]
    col = "llmrr"[p]
    return row + col, q * BLK - ROWS[row][0], p * BLK - COLS[col][0]


def shifted(block, axis, distance):
    n = lax.axis_size(axis)
    return lax.ppermute(block, axis, [((i - distance) % n, i) for i in range(n)])


def around(block, sign):
    rows, cols = lax.axis_size("row"), lax.axis_size("col")
    first, second = [], []
    for row in range(rows):
        for col in range(cols):
            x, z_lo, core = row // 4, row // 2 % 2, row % 2
            y, z_hi = col // 4, col % 4
            z = (2 * z_hi + z_lo - 3 * sign) % 8
            relay = (4 * x + 2 * (z % 2) + core) * cols + 4 * y + z // 2
            first.append((row * cols + col, relay))
            second.append((relay, row * cols + (col + sign) % cols))
    for route in (first, second):
        block = lax.ppermute(block, ("row", "col"), route)
    return block


def split(x):
    hi = x.astype(bf16)
    return hi, (x - hi.astype(f32)).astype(bf16)


def mm(a, b):
    return lax.dot_general(a, b, (((1,), (0,)), ((), ())), preferred_element_type=f32)


def mm_right(x, tab, t):
    hi, lo = split(x)
    return mm(hi, tab[t, 0]) + (mm(hi, tab[t, 1]) + mm(lo, tab[t, 0]))


def mm_left(tab, t, x):
    hi, lo = split(x)
    return mm(tab[t, 0], hi) + (mm(tab[t, 0], lo) + mm(tab[t, 1], hi))


def fft2(re, im, tab):
    k1 = mm_right(re + im, tab, 0)
    k2 = mm_right(re, tab, 1)
    k3 = mm_right(im, tab, 2)
    re, im = k1 - k3, k1 + k2
    k1 = mm_left(tab, 0, re + im)
    k2 = mm_left(tab, 1, re)
    k3 = mm_left(tab, 2, im)
    return k1 - k3, k1 + k2


def ifft2(re, im, tab):
    out_im, out_re = fft2(im, re, tab)
    return out_re, out_im


def times(a, b):
    return a[0] * b[0] - a[1] * b[1], a[0] * b[1] + a[1] * b[0]


def conj_times(a, b):
    return a[0] * b[0] + a[1] * b[1], a[0] * b[1] - a[1] * b[0]


def masks(info, slot, dim):
    corner = info[2 * slot + dim]
    index = lax.broadcasted_iota(jnp.int32, (BLK, BLK), dim)
    out = []
    for q in range(5):
        pixel = index + q * BLK
        out.append((pixel >= corner) & (pixel < corner + WIN))
    return out


def block_rows(slot, q):
    return pl.ds(pl.multiple_of(slot * WIN + (q - 3) * BLK, BLK), BLK)


def pick_columns(cols, pieces, comp, q, g):
    line = None
    for p in range(g, 5, 2):
        name, i, j = locate(q, p)
        block = pieces[name][comp, i:i + BLK, j:j + BLK]
        line = block if line is None else jnp.where(cols[p], block, line)
    return line


def read_window(info, pieces, slot, dst):
    rows, cols = masks(info, slot, 0), masks(info, slot, 1)

    @pl.loop(0, 2)
    def _(comp):
        for h in range(2):
            for g in range(2):
                value = None
                for q in range(h, 5, 2):
                    if q < 3:
                        line = pick_columns(cols, pieces, comp, q, g)
                    else:
                        line = pieces["c"][comp, block_rows(slot, q), g * BLK:(g + 1) * BLK]
                    value = line if value is None else jnp.where(rows[q], line, value)
                dst[comp, h * BLK:(h + 1) * BLK, g * BLK:(g + 1) * BLK] = value


def write_grads(info, grads, outs):
    picks = [(masks(info, slot, 0), masks(info, slot, 1)) for slot in range(SLOTS)]

    @pl.loop(0, 2)
    def _(comp):
        for q in range(3):
            for p in range(5):
                name, i, j = locate(q, p)
                total = None
                for slot in range(SLOTS):
                    rows, cols = picks[slot]
                    r0, c0 = slot * WIN + (q % 2) * BLK, (p % 2) * BLK
                    part = jnp.where(rows[q] & cols[p], grads[comp, r0:r0 + BLK, c0:c0 + BLK], 0.0)
                    total = part if total is None else total + part
                outs[name][comp, i:i + BLK, j:j + BLK] = total * RATE
        for slot in range(SLOTS):
            for q in (3, 4):
                for g in range(2):
                    r0, c0 = slot * WIN + (q % 2) * BLK, g * BLK
                    part = jnp.where(picks[slot][0][q], grads[comp, r0:r0 + BLK, c0:c0 + BLK], 0.0)
                    outs["c"][comp, block_rows(slot, q), c0:c0 + BLK] = part * RATE


def write_picked(above, pieces, picked):
    @pl.loop(0, SLOTS)
    def _(slot):
        cols = masks(above, slot, 1)

        @pl.loop(0, 2)
        def _(comp):
            for q in range(2):
                for g in range(2):
                    picked[comp, block_rows(slot, q + 3), g * BLK:(g + 1) * BLK] = pick_columns(cols, pieces, comp, q, g)


def pick_kernel(above, al, am, ar, picked):
    write_picked(above, {"al": al, "am": am, "ar": ar}, picked)


def sum_kernel(above, below, al, am, ar, *outs):
    grads, outs = {"al": al, "am": am, "ar": ar}, dict(zip(("al", "am", "ar"), outs))
    cols = [masks(above, slot, 1) for slot in range(SLOTS)]

    @pl.loop(0, 4)
    def _(index):
        comp, q = index // 2, index % 2
        rows = pl.ds(pl.multiple_of(q * BLK, BLK), BLK)
        for p in range(5):
            name, _, j = locate(0, p)
            total = grads[name][comp, rows, j:j + BLK]
            for slot in range(SLOTS):
                part = below[comp, block_rows(slot, q + 3), (p % 2) * BLK:(p % 2 + 1) * BLK]
                total = total + jnp.where(cols[slot][p], part, 0.0)
            outs[name][comp, rows, j:j + BLK] = total


def step_kernel(above, al, am, ar, gal, gam, gar, from_left, from_right, *outs):
    new = dict(zip(("al", "am", "ar"), outs))
    new["al"][...] = al[...] - (gal[...] + from_left[...])
    new["am"][...] = am[...] - gam[...]
    new["ar"][...] = ar[:, :WIN] - (gar[...] + from_right[...])
    write_picked(above, new, outs[3])


def setup_kernel(info, probe, trig, rolled, tab):
    for slot in range(SLOTS):
        for comp in range(2):
            turned = pltpu.roll(probe[comp], lax.rem(info[2 * slot], WIN), 0)
            rolled[comp, slot * WIN:(slot + 1) * WIN, :] = pltpu.roll(turned, lax.rem(info[2 * slot + 1], WIN), 1)
    cosine, sine = trig[0] / math.sqrt(WIN), trig[1] / math.sqrt(WIN)
    for t, table in enumerate([cosine, -(cosine + sine), cosine - sine]):
        tab[t, 0], tab[t, 1] = split(table)


def slot_rows(slot):
    return pl.ds(pl.multiple_of(slot * WIN, WIN), WIN)


def psi_kernel(info, probe, trig, tab, *refs):
    pieces = dict(zip(NAMES, refs[:7]))
    psi, window = refs[7], refs[8]

    @pl.loop(0, SLOTS)
    def _(slot):
        rows = slot_rows(slot)
        read_window(info, pieces, slot, window)
        field = times((probe[0, rows], probe[1, rows]), (window[0], window[1]))
        field = times((trig[2], trig[3]), fft2(*field, tab))
        psi[0, rows], psi[1, rows] = ifft2(*field, tab)


def exit_kernel(info, psi, measured, tab, *refs):
    pieces = dict(zip(NAMES, refs[:7]))
    outs = dict(zip(NAMES, refs[7:14]))
    back, window, grads = refs[14], refs[15], refs[16]

    @pl.loop(0, SLOTS)
    def _(slot):
        rows = slot_rows(slot)
        live = (slot < info[4]).astype(f32)
        read_window(info, pieces, slot, window)
        far = fft2(*times((psi[0, rows], psi[1, rows]), (window[0], window[1])), tab)
        misfit = live * (far[0] * far[0] + far[1] * far[1] - measured[rows])
        leave = ifft2(misfit * far[0], misfit * far[1], tab)
        grads[0, rows], grads[1, rows] = conj_times((psi[0, rows], psi[1, rows]), leave)
        back[0, rows], back[1, rows] = conj_times((window[0], window[1]), leave)

    write_grads(info, grads, outs)


def back_kernel(info, probe, trig, back, tab, *refs):
    outs = dict(zip(NAMES, refs[:7]))
    grads = refs[7]

    @pl.loop(0, SLOTS)
    def _(slot):
        rows = slot_rows(slot)
        field = conj_times((trig[2], trig[3]), fft2(back[0, rows], back[1, rows], tab))
        field = ifft2(*field, tab)
        grads[0, rows], grads[1, rows] = conj_times((probe[0, rows], probe[1, rows]), field)

    write_grads(info, grads, outs)


smem = pl.BlockSpec(memory_space=pltpu.SMEM)
vmem = pl.BlockSpec(memory_space=pltpu.VMEM)
scratch = pltpu.VMEM(STACKED, f32)
window = pltpu.VMEM((2, WIN, WIN), f32)
INTERPRET = False


def call(kernel, shapes, scratches=()):
    def run(info, *rest):
        if not INTERPRET:
            rest = [pltpu.with_memory_space_constraint(x, pltpu.VMEM) for x in rest]
        return pl.pallas_call(
            kernel,
            out_shape=[pltpu.VMEM(s, d) for s, d in shapes],
            in_specs=[smem] + [vmem] * len(rest),
            out_specs=[vmem] * len(shapes),
            scratch_shapes=list(scratches),
            interpret=INTERPRET,
            compiler_params=pltpu.CompilerParams(vmem_limit_bytes=24 << 20),
        )(info, *rest)

    return run


def run(object_field, probe_wave, prop_phase, corners, counts, intensities):
    info = jnp.concatenate([corners.reshape(-1), counts.reshape(-1)])
    measured = intensities.reshape(SLOTS * WIN, WIN)
    field = (STACKED, f32)
    region = [(piece_shape(n), f32) for n in NAMES]
    top = ("al", "am", "ar")

    now = []
    for s in range(2):
        tile = object_field[s]
        now.append({
            n: lax.slice(tile, (0, ROWS[n[0]][0], COLS[n[1]][0]), (2, ROWS[n[0]][1], COLS[n[1]][1]))
            for n in ("al", "am", "bl", "bm")
        })
    part = 96
    rest = now[0]["bl"].shape[1] - part
    relayed = around(jnp.concatenate([now[0]["bl"][:, part:], now[1]["bl"]], 1), -1)
    now[1]["br"] = relayed[:, rest:]
    above = shifted(corners.reshape(-1), "row", 1)
    for s, x in enumerate(now):
        source = x["al"] if s else object_field[0, :, :WIN + part, :WIN]
        x["ar"] = shifted(source, "col", -1)
        (picked,) = call(pick_kernel, [field])(above, *[x[n] for n in top])
        x["c"] = shifted(picked, "row", -1)

    now[0]["br"] = jnp.concatenate([now[0]["ar"][:, WIN:], relayed[:, :rest]], 1)

    index = lax.iota(jnp.int32, WIN)
    product = index[:, None] * index[None, :] + jnp.array([WIN, 3 * WIN // 4], jnp.int32)[:, None, None]
    angles = (product % WIN).astype(f32) * (2.0 * math.pi / WIN)
    trig = jnp.cos(jnp.concatenate([angles, jnp.stack([prop_phase, prop_phase - math.pi / 2])]))
    rolled, tab = call(setup_kernel, [field, ((3, 2, WIN, WIN), bf16)])(info, probe_wave, trig)

    for step in range(STEPS):
        last = step == STEPS - 1
        (psi,) = call(psi_kernel, [field], [window])(
            info, rolled, trig, tab, *[now[0][n] for n in NAMES])
        *grads2, back = call(exit_kernel, region + [field], [window, scratch])(
            info, psi, measured, tab, *[now[1][n] for n in NAMES])
        grads1 = call(back_kernel, region, [scratch])(info, rolled, trig, back, tab)
        grads = [dict(zip(NAMES, grads1)), dict(zip(NAMES, grads2))]
        if last:
            relayed = around(jnp.concatenate([grads[0]["br"][:, part:], grads[1]["br"]], 1), 1)
            direct = shifted(grads[0]["br"][:, :part], "col", 1)
            left_b = [jnp.concatenate([direct, relayed[:, :rest]], 1), relayed[:, rest:]]
        for s in (1, 0):
            x, g = now[s], grads[s]
            found = shifted(g["c"], "row", 1)
            al, am, ar = call(sum_kernel, region[:3])(above, found, *[g[n] for n in top])
            left_a = shifted(ar, "col", 1)
            new = {"bm": x["bm"] - g["bm"]}
            if last:
                new["al"] = x["al"] - (al + left_a)
                new["am"] = x["am"] - am
                new["bl"] = x["bl"] - (g["bl"] + left_b[s])
            else:
                right_a = shifted(al, "col", -1)
                new["bl"] = x["bl"] - (g["bl"] + shifted(g["br"], "col", 1))
                new["br"] = x["br"] - (g["br"] + shifted(g["bl"], "col", -1))
                new["al"], new["am"], new["ar"], picked = call(step_kernel, region[:3] + [field])(
                    above, *[x[n] for n in top], al, am, ar, left_a, right_a)
                new["c"] = shifted(picked, "row", -1)
            now[s] = new
    return jnp.stack([
        jnp.concatenate([
            jnp.concatenate([x["al"], x["am"]], 2),
            jnp.concatenate([x["bl"], x["bm"]], 2),
        ], 1)
        for x in now
    ])


def solution(mesh):
    return jax.shard_map(
        run,
        mesh=mesh,
        in_specs=(
            P(None, None, "row", "col"),
            P(),
            P(),
            P("row", "col", None, None),
            P("row", "col"),
            P("row", "col", None, None, None),
        ),
        out_specs=P(None, None, "row", "col"),
        check_vma=False,
    )
```

```python
import math

import jax
import jax.numpy as jnp
from jax import lax
from jax.experimental import pallas as pl
from jax.experimental.pallas import tpu as pltpu
from jax.sharding import PartitionSpec as P


STEPS = 2
RATE = 0.1
WIN = 256
BLK = 128
SLOTS = 2
f32 = jnp.float32
bf16 = jnp.bfloat16

ROWS = {"a": (0, 256), "b": (256, 384)}
COLS = {"l": (0, 256), "m": (256, 384), "r": (384, 640)}
NAMES = ["al", "am", "ar", "bl", "bm", "br", "c"]
STACKED = (2, SLOTS * WIN, WIN)


def piece_shape(name):
    if name == "c":
        return STACKED
    r, c = ROWS[name[0]], COLS[name[1]]
    return (2, r[1] - r[0], c[1] - c[0])


def locate(q, p):
    row = "aab"[q]
    col = "llmrr"[p]
    return row + col, q * BLK - ROWS[row][0], p * BLK - COLS[col][0]


def shifted(block, axis, distance):
    n = lax.axis_size(axis)
    return lax.ppermute(block, axis, [((i - distance) % n, i) for i in range(n)])


def around(block, sign):
    rows, cols = lax.axis_size("row"), lax.axis_size("col")
    first, second = [], []
    for row in range(rows):
        for col in range(cols):
            x, z_lo, core = row // 4, row // 2 % 2, row % 2
            y, z_hi = col // 4, col % 4
            z = (2 * z_hi + z_lo - 3 * sign) % 8
            relay = (4 * x + 2 * (z % 2) + core) * cols + 4 * y + z // 2
            first.append((row * cols + col, relay))
            second.append((relay, row * cols + (col + sign) % cols))
    for route in (first, second):
        block = lax.ppermute(block, ("row", "col"), route)
    return block


def split(x):
    hi = x.astype(bf16)
    return hi, (x - hi.astype(f32)).astype(bf16)


def mm(a, b):
    return lax.dot_general(a, b, (((1,), (0,)), ((), ())), preferred_element_type=f32)


def mm_right(x, tab, t):
    hi, lo = split(x)
    return mm(hi, tab[t, 0]) + (mm(hi, tab[t, 1]) + mm(lo, tab[t, 0]))


def mm_left(tab, t, x):
    hi, lo = split(x)
    return mm(tab[t, 0], hi) + (mm(tab[t, 0], lo) + mm(tab[t, 1], hi))


def fft2(re, im, tab):
    k1 = mm_right(re + im, tab, 0)
    k2 = mm_right(re, tab, 1)
    k3 = mm_right(im, tab, 2)
    re, im = k1 - k3, k1 + k2
    k1 = mm_left(tab, 0, re + im)
    k2 = mm_left(tab, 1, re)
    k3 = mm_left(tab, 2, im)
    return k1 - k3, k1 + k2


def ifft2(re, im, tab):
    out_im, out_re = fft2(im, re, tab)
    return out_re, out_im


def times(a, b):
    return a[0] * b[0] - a[1] * b[1], a[0] * b[1] + a[1] * b[0]


def conj_times(a, b):
    return a[0] * b[0] + a[1] * b[1], a[0] * b[1] - a[1] * b[0]


def masks(info, slot, dim):
    corner = info[2 * slot + dim]
    index = lax.broadcasted_iota(jnp.int32, (BLK, BLK), dim)
    out = []
    for q in range(5):
        pixel = index + q * BLK
        out.append((pixel >= corner) & (pixel < corner + WIN))
    return out


def block_rows(slot, q):
    return pl.ds(pl.multiple_of(slot * WIN + (q - 3) * BLK, BLK), BLK)


def pick_columns(cols, pieces, comp, q, g):
    line = None
    for p in range(g, 5, 2):
        name, i, j = locate(q, p)
        block = pieces[name][comp, i:i + BLK, j:j + BLK]
        line = block if line is None else jnp.where(cols[p], block, line)
    return line


def read_window(info, pieces, slot, dst):
    rows, cols = masks(info, slot, 0), masks(info, slot, 1)

    @pl.loop(0, 2)
    def _(comp):
        for h in range(2):
            for g in range(2):
                value = None
                for q in range(h, 5, 2):
                    if q < 3:
                        line = pick_columns(cols, pieces, comp, q, g)
                    else:
                        line = pieces["c"][comp, block_rows(slot, q), g * BLK:(g + 1) * BLK]
                    value = line if value is None else jnp.where(rows[q], line, value)
                dst[comp, h * BLK:(h + 1) * BLK, g * BLK:(g + 1) * BLK] = value


def write_grads(info, grads, outs):
    picks = [(masks(info, slot, 0), masks(info, slot, 1)) for slot in range(SLOTS)]

    @pl.loop(0, 2)
    def _(comp):
        for q in range(3):
            for p in range(5):
                name, i, j = locate(q, p)
                total = None
                for slot in range(SLOTS):
                    rows, cols = picks[slot]
                    r0, c0 = slot * WIN + (q % 2) * BLK, (p % 2) * BLK
                    part = jnp.where(rows[q] & cols[p], grads[comp, r0:r0 + BLK, c0:c0 + BLK], 0.0)
                    total = part if total is None else total + part
                outs[name][comp, i:i + BLK, j:j + BLK] = total * RATE
        for slot in range(SLOTS):
            for q in (3, 4):
                for g in range(2):
                    r0, c0 = slot * WIN + (q % 2) * BLK, g * BLK
                    part = jnp.where(picks[slot][0][q], grads[comp, r0:r0 + BLK, c0:c0 + BLK], 0.0)
                    outs["c"][comp, block_rows(slot, q), c0:c0 + BLK] = part * RATE


def write_picked(above, pieces, picked):
    @pl.loop(0, SLOTS)
    def _(slot):
        cols = masks(above, slot, 1)

        @pl.loop(0, 2)
        def _(comp):
            for q in range(2):
                for g in range(2):
                    picked[comp, block_rows(slot, q + 3), g * BLK:(g + 1) * BLK] = pick_columns(cols, pieces, comp, q, g)


def pick_kernel(above, al, am, ar, picked):
    write_picked(above, {"al": al, "am": am, "ar": ar}, picked)


def sum_kernel(above, below, al, am, ar, *refs):
    grads, outs = {"al": al, "am": am, "ar": ar}, dict(zip(("al", "am", "ar"), refs[-3:]))
    if len(refs) == 4:
        outs["ar"][:, WIN:] = refs[0][:, :outs["ar"].shape[1] - WIN]
    cols = [masks(above, slot, 1) for slot in range(SLOTS)]

    @pl.loop(0, 4)
    def _(index):
        comp, q = index // 2, index % 2
        rows = pl.ds(pl.multiple_of(q * BLK, BLK), BLK)
        for p in range(5):
            name, _, j = locate(0, p)
            total = grads[name][comp, rows, j:j + BLK]
            for slot in range(SLOTS):
                part = below[comp, block_rows(slot, q + 3), (p % 2) * BLK:(p % 2 + 1) * BLK]
                total = total + jnp.where(cols[slot][p], part, 0.0)
            outs[name][comp, rows, j:j + BLK] = total


def step_kernel(above, al, am, ar, gal, gam, gar, from_left, from_right, *outs):
    new = dict(zip(("al", "am", "ar"), outs))
    new["al"][...] = al[...] - (gal[...] + from_left[...])
    new["am"][...] = am[...] - gam[...]
    new["ar"][...] = ar[:, :WIN] - (gar[...] + from_right[...])
    write_picked(above, new, outs[3])


def setup_kernel(info, probe, trig, rolled, tab):
    for slot in range(SLOTS):
        for comp in range(2):
            turned = pltpu.roll(probe[comp], lax.rem(info[2 * slot], WIN), 0)
            rolled[comp, slot * WIN:(slot + 1) * WIN, :] = pltpu.roll(turned, lax.rem(info[2 * slot + 1], WIN), 1)
    cosine, sine = trig[0] / math.sqrt(WIN), trig[1] / math.sqrt(WIN)
    for t, table in enumerate([cosine, -(cosine + sine), cosine - sine]):
        tab[t, 0], tab[t, 1] = split(table)


def slot_rows(slot):
    return pl.ds(pl.multiple_of(slot * WIN, WIN), WIN)


def psi_kernel(info, probe, trig, tab, *refs):
    pieces = dict(zip(NAMES, refs[:7]))
    psi, window = refs[7], refs[8]

    @pl.loop(0, SLOTS)
    def _(slot):
        rows = slot_rows(slot)
        read_window(info, pieces, slot, window)
        field = times((probe[0, rows], probe[1, rows]), (window[0], window[1]))
        field = times((trig[2], trig[3]), fft2(*field, tab))
        psi[0, rows], psi[1, rows] = ifft2(*field, tab)


def exit_kernel(info, psi, measured, tab, *refs):
    pieces = dict(zip(NAMES, refs[:7]))
    outs = dict(zip(NAMES, refs[7:14]))
    back, window, grads = refs[14], refs[15], refs[16]

    @pl.loop(0, SLOTS)
    def _(slot):
        rows = slot_rows(slot)
        live = (slot < info[4]).astype(f32)
        read_window(info, pieces, slot, window)
        far = fft2(*times((psi[0, rows], psi[1, rows]), (window[0], window[1])), tab)
        misfit = live * (far[0] * far[0] + far[1] * far[1] - measured[rows])
        leave = ifft2(misfit * far[0], misfit * far[1], tab)
        grads[0, rows], grads[1, rows] = conj_times((psi[0, rows], psi[1, rows]), leave)
        back[0, rows], back[1, rows] = conj_times((window[0], window[1]), leave)

    write_grads(info, grads, outs)


def back_kernel(info, probe, trig, back, tab, *refs):
    outs = dict(zip(NAMES, refs[:7]))
    grads = refs[7]

    @pl.loop(0, SLOTS)
    def _(slot):
        rows = slot_rows(slot)
        field = conj_times((trig[2], trig[3]), fft2(back[0, rows], back[1, rows], tab))
        field = ifft2(*field, tab)
        grads[0, rows], grads[1, rows] = conj_times((probe[0, rows], probe[1, rows]), field)

    write_grads(info, grads, outs)


smem = pl.BlockSpec(memory_space=pltpu.SMEM)
vmem = pl.BlockSpec(memory_space=pltpu.VMEM)
scratch = pltpu.VMEM(STACKED, f32)
window = pltpu.VMEM((2, WIN, WIN), f32)
INTERPRET = False


def call(kernel, shapes, scratches=()):
    def run(info, *rest):
        if not INTERPRET:
            rest = [pltpu.with_memory_space_constraint(x, pltpu.VMEM) for x in rest]
        return pl.pallas_call(
            kernel,
            out_shape=[pltpu.VMEM(s, d) for s, d in shapes],
            in_specs=[smem] + [vmem] * len(rest),
            out_specs=[vmem] * len(shapes),
            scratch_shapes=list(scratches),
            interpret=INTERPRET,
            compiler_params=pltpu.CompilerParams(vmem_limit_bytes=24 << 20),
        )(info, *rest)

    return run


def run(object_field, probe_wave, prop_phase, corners, counts, intensities):
    info = jnp.concatenate([corners.reshape(-1), counts.reshape(-1)])
    measured = intensities.reshape(SLOTS * WIN, WIN)
    field = (STACKED, f32)
    region = [(piece_shape(n), f32) for n in NAMES]
    top = ("al", "am", "ar")

    def cut(s, rows, cols):
        block = lax.slice(object_field, (s, 0, rows[0], cols[0]), (s + 1, 2, rows[1], cols[1]))
        return block.reshape(block.shape[1:])

    now = []
    for s in range(2):
        now.append({n: cut(s, ROWS[n[0]], COLS[n[1]]) for n in ("al", "am", "bl", "bm")})
    part = 96
    rest = now[0]["bl"].shape[1] - part
    relayed = around(jnp.concatenate([now[0]["bl"][:, part:], now[1]["bl"]], 1), -1)
    now[1]["br"] = relayed[:, rest:]
    above = shifted(corners.reshape(-1), "row", 1)
    for s, x in enumerate(now):
        source = x["al"] if s else cut(0, (0, WIN + part), (0, WIN))
        x["ar"] = shifted(source, "col", -1)
        (picked,) = call(pick_kernel, [field])(above, *[x[n] for n in top])
        x["c"] = shifted(picked, "row", -1)

    now[0]["br"] = jnp.concatenate([now[0]["ar"][:, WIN:], relayed[:, :rest]], 1)

    index = lax.iota(jnp.int32, WIN)
    product = index[:, None] * index[None, :] + jnp.array([WIN, 3 * WIN // 4], jnp.int32)[:, None, None]
    angles = (product % WIN).astype(f32) * (2.0 * math.pi / WIN)
    trig = jnp.cos(jnp.concatenate([angles, jnp.stack([prop_phase, prop_phase - math.pi / 2])]))
    rolled, tab = call(setup_kernel, [field, ((3, 2, WIN, WIN), bf16)])(info, probe_wave, trig)

    for step in range(STEPS):
        last = step == STEPS - 1
        (psi,) = call(psi_kernel, [field], [window])(
            info, rolled, trig, tab, *[now[0][n] for n in NAMES])
        *grads2, back = call(exit_kernel, region + [field], [window, scratch])(
            info, psi, measured, tab, *[now[1][n] for n in NAMES])
        grads1 = call(back_kernel, region, [scratch])(info, rolled, trig, back, tab)
        grads = [dict(zip(NAMES, grads1)), dict(zip(NAMES, grads2))]
        if last:
            relayed = around(jnp.concatenate([grads[0]["br"][:, part:], grads[1]["br"]], 1), 1)
        for s in (1, 0):
            x, g = now[s], grads[s]
            found = shifted(g["c"], "row", 1)
            shapes, extra = region[:3], []
            if last and s == 0:
                shapes, extra = region[:2] + [((2, WIN + part, WIN), f32)], [g["br"]]
            al, am, ar = call(sum_kernel, shapes)(above, found, *[g[n] for n in top], *extra)
            left_a = shifted(ar, "col", 1)
            new = {"bm": x["bm"] - g["bm"]}
            if last:
                left_b = relayed[:, rest:] if s else jnp.concatenate([left_a[:, WIN:], relayed[:, :rest]], 1)
                new["al"] = x["al"] - (al + left_a[:, :WIN])
                new["am"] = x["am"] - am
                new["bl"] = x["bl"] - (g["bl"] + left_b)
            else:
                right_a = shifted(al, "col", -1)
                new["bl"] = x["bl"] - (g["bl"] + shifted(g["br"], "col", 1))
                new["br"] = x["br"] - (g["br"] + shifted(g["bl"], "col", -1))
                new["al"], new["am"], new["ar"], picked = call(step_kernel, region[:3] + [field])(
                    above, *[x[n] for n in top], al, am, ar, left_a, right_a)
                new["c"] = shifted(picked, "row", -1)
            now[s] = new
    return jnp.stack([
        jnp.concatenate([
            jnp.concatenate([x["al"], x["am"]], 2),
            jnp.concatenate([x["bl"], x["bm"]], 2),
        ], 1)
        for x in now
    ])


def solution(mesh):
    return jax.shard_map(
        run,
        mesh=mesh,
        in_specs=(
            P(None, None, "row", "col"),
            P(),
            P(),
            P("row", "col", None, None),
            P("row", "col"),
            P("row", "col", None, None, None),
        ),
        out_specs=P(None, None, "row", "col"),
        check_vma=False,
    )
```

```python
import math

import jax
import jax.numpy as jnp
from jax import lax
from jax.experimental import pallas as pl
from jax.experimental.pallas import tpu as pltpu
from jax.sharding import PartitionSpec as P


STEPS = 2
RATE = 0.1
WIN = 256
BLK = 128
SLOTS = 2
f32 = jnp.float32
bf16 = jnp.bfloat16

ROWS = {"a": (0, 256), "b": (256, 384)}
COLS = {"l": (0, 256), "m": (256, 384), "r": (384, 640)}
NAMES = ["al", "am", "ar", "bl", "bm", "br", "c"]
STACKED = (2, SLOTS * WIN, WIN)


def piece_shape(name):
    if name == "c":
        return STACKED
    r, c = ROWS[name[0]], COLS[name[1]]
    return (2, r[1] - r[0], c[1] - c[0])


def locate(q, p):
    row = "aab"[q]
    col = "llmrr"[p]
    return row + col, q * BLK - ROWS[row][0], p * BLK - COLS[col][0]


def shifted(block, axis, distance):
    n = lax.axis_size(axis)
    return lax.ppermute(block, axis, [((i - distance) % n, i) for i in range(n)])


def around(block, sign):
    rows, cols = lax.axis_size("row"), lax.axis_size("col")
    first, second = [], []
    for row in range(rows):
        for col in range(cols):
            x, z_lo, core = row // 4, row // 2 % 2, row % 2
            y, z_hi = col // 4, col % 4
            z = (2 * z_hi + z_lo - 3 * sign) % 8
            relay = (4 * x + 2 * (z % 2) + core) * cols + 4 * y + z // 2
            first.append((row * cols + col, relay))
            second.append((relay, row * cols + (col + sign) % cols))
    for route in (first, second):
        block = lax.ppermute(block, ("row", "col"), route)
    return block


def split(x):
    hi = x.astype(bf16)
    return hi, (x - hi.astype(f32)).astype(bf16)


def mm(a, b):
    return lax.dot_general(a, b, (((1,), (0,)), ((), ())), preferred_element_type=f32)


def mm_right(x, tab, t):
    hi, lo = split(x)
    return mm(hi, tab[t, 0]) + (mm(hi, tab[t, 1]) + mm(lo, tab[t, 0]))


def mm_left(tab, t, x):
    hi, lo = split(x)
    return mm(tab[t, 0], hi) + (mm(tab[t, 0], lo) + mm(tab[t, 1], hi))


def fft2(re, im, tab):
    k1 = mm_right(re + im, tab, 0)
    k2 = mm_right(re, tab, 1)
    k3 = mm_right(im, tab, 2)
    re, im = k1 - k3, k1 + k2
    k1 = mm_left(tab, 0, re + im)
    k2 = mm_left(tab, 1, re)
    k3 = mm_left(tab, 2, im)
    return k1 - k3, k1 + k2


def ifft2(re, im, tab):
    out_im, out_re = fft2(im, re, tab)
    return out_re, out_im


def times(a, b):
    return a[0] * b[0] - a[1] * b[1], a[0] * b[1] + a[1] * b[0]


def conj_times(a, b):
    return a[0] * b[0] + a[1] * b[1], a[0] * b[1] - a[1] * b[0]


def masks(info, slot, dim):
    corner = info[2 * slot + dim]
    index = lax.broadcasted_iota(jnp.int32, (BLK, BLK), dim)
    out = []
    for q in range(5):
        pixel = index + q * BLK
        out.append((pixel >= corner) & (pixel < corner + WIN))
    return out


def block_rows(slot, q):
    return pl.ds(pl.multiple_of(slot * WIN + (q - 3) * BLK, BLK), BLK)


def pick_columns(cols, pieces, comp, q, g):
    line = None
    for p in range(g, 5, 2):
        name, i, j = locate(q, p)
        block = pieces[name][comp, i:i + BLK, j:j + BLK]
        line = block if line is None else jnp.where(cols[p], block, line)
    return line


def read_window(info, pieces, slot, dst):
    rows, cols = masks(info, slot, 0), masks(info, slot, 1)

    @pl.loop(0, 2)
    def _(comp):
        for h in range(2):
            for g in range(2):
                value = None
                for q in range(h, 5, 2):
                    if q < 3:
                        line = pick_columns(cols, pieces, comp, q, g)
                    else:
                        line = pieces["c"][comp, block_rows(slot, q), g * BLK:(g + 1) * BLK]
                    value = line if value is None else jnp.where(rows[q], line, value)
                dst[comp, h * BLK:(h + 1) * BLK, g * BLK:(g + 1) * BLK] = value


def write_grads(info, grads, outs):
    picks = [(masks(info, slot, 0), masks(info, slot, 1)) for slot in range(SLOTS)]

    @pl.loop(0, 2)
    def _(comp):
        for q in range(3):
            for p in range(5):
                name, i, j = locate(q, p)
                total = None
                for slot in range(SLOTS):
                    rows, cols = picks[slot]
                    r0, c0 = slot * WIN + (q % 2) * BLK, (p % 2) * BLK
                    part = jnp.where(rows[q] & cols[p], grads[comp, r0:r0 + BLK, c0:c0 + BLK], 0.0)
                    total = part if total is None else total + part
                outs[name][comp, i:i + BLK, j:j + BLK] = total * RATE
        for slot in range(SLOTS):
            for q in (3, 4):
                for g in range(2):
                    r0, c0 = slot * WIN + (q % 2) * BLK, g * BLK
                    part = jnp.where(picks[slot][0][q], grads[comp, r0:r0 + BLK, c0:c0 + BLK], 0.0)
                    outs["c"][comp, block_rows(slot, q), c0:c0 + BLK] = part * RATE


def write_picked(above, pieces, picked):
    @pl.loop(0, SLOTS)
    def _(slot):
        cols = masks(above, slot, 1)

        @pl.loop(0, 2)
        def _(comp):
            for q in range(2):
                for g in range(2):
                    picked[comp, block_rows(slot, q + 3), g * BLK:(g + 1) * BLK] = pick_columns(cols, pieces, comp, q, g)


def pick_kernel(above, al, am, ar, picked):
    write_picked(above, {"al": al, "am": am, "ar": ar}, picked)


def sum_kernel(above, below, al, am, ar, *refs):
    grads, outs = {"al": al, "am": am, "ar": ar}, dict(zip(("al", "am", "ar"), refs[-3:]))
    if len(refs) == 4:
        outs["ar"][:, WIN:] = refs[0][:, :outs["ar"].shape[1] - WIN]
    cols = [masks(above, slot, 1) for slot in range(SLOTS)]

    @pl.loop(0, 4)
    def _(index):
        comp, q = index // 2, index % 2
        rows = pl.ds(pl.multiple_of(q * BLK, BLK), BLK)
        for p in range(5):
            name, _, j = locate(0, p)
            total = grads[name][comp, rows, j:j + BLK]
            for slot in range(SLOTS):
                part = below[comp, block_rows(slot, q + 3), (p % 2) * BLK:(p % 2 + 1) * BLK]
                total = total + jnp.where(cols[slot][p], part, 0.0)
            outs[name][comp, rows, j:j + BLK] = total


def step_kernel(above, al, am, ar, gal, gam, gar, from_left, from_right, *outs):
    new = dict(zip(("al", "am", "ar"), outs))
    new["al"][...] = al[...] - (gal[...] + from_left[...])
    new["am"][...] = am[...] - gam[...]
    new["ar"][...] = ar[:, :WIN] - (gar[...] + from_right[...])
    write_picked(above, new, outs[3])


def setup_kernel(info, probe, trig, rolled, tab):
    for slot in range(SLOTS):
        for comp in range(2):
            turned = pltpu.roll(probe[comp], lax.rem(info[2 * slot], WIN), 0)
            rolled[comp, slot * WIN:(slot + 1) * WIN, :] = pltpu.roll(turned, lax.rem(info[2 * slot + 1], WIN), 1)
    cosine, sine = trig[0] / math.sqrt(WIN), trig[1] / math.sqrt(WIN)
    for t, table in enumerate([cosine, -(cosine + sine), cosine - sine]):
        tab[t, 0], tab[t, 1] = split(table)


def slot_rows(slot):
    return pl.ds(pl.multiple_of(slot * WIN, WIN), WIN)


def psi_kernel(info, probe, trig, tab, *refs):
    pieces = dict(zip(NAMES, refs[:7]))
    psi, window = refs[7], refs[8]

    @pl.loop(0, SLOTS)
    def _(slot):
        rows = slot_rows(slot)
        read_window(info, pieces, slot, window)
        field = times((probe[0, rows], probe[1, rows]), (window[0], window[1]))
        field = times((trig[2], trig[3]), fft2(*field, tab))
        psi[0, rows], psi[1, rows] = ifft2(*field, tab)


def exit_kernel(info, psi, measured, tab, *refs):
    pieces = dict(zip(NAMES, refs[:7]))
    outs = dict(zip(NAMES, refs[7:14]))
    back, window, grads = refs[14], refs[15], refs[16]

    @pl.loop(0, SLOTS)
    def _(slot):
        rows = slot_rows(slot)
        live = (slot < info[4]).astype(f32)
        read_window(info, pieces, slot, window)
        far = fft2(*times((psi[0, rows], psi[1, rows]), (window[0], window[1])), tab)
        misfit = live * (far[0] * far[0] + far[1] * far[1] - measured[rows])
        leave = ifft2(misfit * far[0], misfit * far[1], tab)
        grads[0, rows], grads[1, rows] = conj_times((psi[0, rows], psi[1, rows]), leave)
        back[0, rows], back[1, rows] = conj_times((window[0], window[1]), leave)

    write_grads(info, grads, outs)


def back_kernel(info, probe, trig, back, tab, *refs):
    outs = dict(zip(NAMES, refs[:7]))
    grads = refs[7]

    @pl.loop(0, SLOTS)
    def _(slot):
        rows = slot_rows(slot)
        field = conj_times((trig[2], trig[3]), fft2(back[0, rows], back[1, rows], tab))
        field = ifft2(*field, tab)
        grads[0, rows], grads[1, rows] = conj_times((probe[0, rows], probe[1, rows]), field)

    write_grads(info, grads, outs)


smem = pl.BlockSpec(memory_space=pltpu.SMEM)
vmem = pl.BlockSpec(memory_space=pltpu.VMEM)
scratch = pltpu.VMEM(STACKED, f32)
window = pltpu.VMEM((2, WIN, WIN), f32)
INTERPRET = False


def call(kernel, shapes, scratches=()):
    def run(info, *rest):
        if not INTERPRET:
            rest = [pltpu.with_memory_space_constraint(x, pltpu.VMEM) for x in rest]
        return pl.pallas_call(
            kernel,
            out_shape=[pltpu.VMEM(s, d) for s, d in shapes],
            in_specs=[smem] + [vmem] * len(rest),
            out_specs=[vmem] * len(shapes),
            scratch_shapes=list(scratches),
            interpret=INTERPRET,
            compiler_params=pltpu.CompilerParams(vmem_limit_bytes=24 << 20),
        )(info, *rest)

    return run


def run(object_field, probe_wave, prop_phase, corners, counts, intensities):
    info = jnp.concatenate([corners.reshape(-1), counts.reshape(-1)])
    measured = intensities.reshape(SLOTS * WIN, WIN)
    field = (STACKED, f32)
    region = [(piece_shape(n), f32) for n in NAMES]
    top = ("al", "am", "ar")

    def cut(s, rows, cols):
        block = lax.slice(object_field, (s, 0, rows[0], cols[0]), (s + 1, 2, rows[1], cols[1]))
        return block.reshape(block.shape[1:])

    now = []
    for s in range(2):
        now.append({n: cut(s, ROWS[n[0]], COLS[n[1]]) for n in ("al", "am", "bl", "bm")})
    part = 96
    rest = now[0]["bl"].shape[1] - part
    relayed = around(jnp.concatenate([now[0]["bl"][:, part:], now[1]["bl"]], 1), -1)
    now[1]["br"] = relayed[:, rest:]
    above = shifted(corners.reshape(-1), "row", 1)
    for s, x in enumerate(now):
        source = x["al"] if s else cut(0, (0, WIN + part), (0, WIN))
        x["ar"] = shifted(source, "col", -1)
        (picked,) = call(pick_kernel, [field])(above, *[x[n] for n in top])
        x["c"] = shifted(picked, "row", -1)

    now[0]["br"] = jnp.concatenate([now[0]["ar"][:, WIN:], relayed[:, :rest]], 1)

    index = lax.iota(jnp.int32, WIN)
    product = index[:, None] * index[None, :] + jnp.array([WIN, 3 * WIN // 4], jnp.int32)[:, None, None]
    angles = (product % WIN).astype(f32) * (2.0 * math.pi / WIN)
    trig = jnp.cos(jnp.concatenate([angles, jnp.stack([prop_phase, prop_phase - math.pi / 2])]))
    rolled, tab = call(setup_kernel, [field, ((3, 2, WIN, WIN), bf16)])(info, probe_wave, trig)

    for step in range(STEPS):
        last = step == STEPS - 1
        (psi,) = call(psi_kernel, [field], [window])(
            info, rolled, trig, tab, *[now[0][n] for n in NAMES])
        *grads2, back = call(exit_kernel, region + [field], [window, scratch])(
            info, psi, measured, tab, *[now[1][n] for n in NAMES])
        grads1 = call(back_kernel, region, [scratch])(info, rolled, trig, back, tab)
        grads = [dict(zip(NAMES, grads1)), dict(zip(NAMES, grads2))]
        if last:
            relayed = around(jnp.concatenate([grads[0]["br"][:, part:], grads[1]["br"]], 1), 1)
        low = {}
        for s in (1, 0):
            x, g = now[s], grads[s]
            found = shifted(g["c"], "row", 1)
            shapes, extra = region[:3], []
            if last and s == 0:
                shapes, extra = region[:2] + [((2, WIN + part, WIN), f32)], [g["br"]]
            al, am, ar = call(sum_kernel, shapes)(above, found, *[g[n] for n in top], *extra)
            left_a = shifted(ar, "col", 1)
            new = {"bm": x["bm"] - g["bm"]}
            if last:
                left_b = relayed[:, rest:] if s else jnp.concatenate([left_a[:, WIN:], relayed[:, :rest]], 1)
                new["al"] = x["al"] - (al + left_a[:, :WIN])
                new["am"] = x["am"] - am
                new["bl"] = x["bl"] - (g["bl"] + left_b)
            else:
                right_a = shifted(al, "col", -1)
                low[s] = (x, g, shifted(g["br"], "col", 1), shifted(g["bl"], "col", -1))
                new["al"], new["am"], new["ar"], picked = call(step_kernel, region[:3] + [field])(
                    above, *[x[n] for n in top], al, am, ar, left_a, right_a)
                new["c"] = shifted(picked, "row", -1)
            now[s] = new
        for s in sorted(low):
            x, g, from_left, from_right = low[s]
            if s:
                from_left, from_right, _ = lax.optimization_barrier((from_left, from_right, now[0]["bl"]))
            now[s]["bl"] = x["bl"] - (g["bl"] + from_left)
            now[s]["br"] = x["br"] - (g["br"] + from_right)
    return jnp.stack([
        jnp.concatenate([
            jnp.concatenate([x["al"], x["am"]], 2),
            jnp.concatenate([x["bl"], x["bm"]], 2),
        ], 1)
        for x in now
    ])


def solution(mesh):
    return jax.shard_map(
        run,
        mesh=mesh,
        in_specs=(
            P(None, None, "row", "col"),
            P(),
            P(),
            P("row", "col", None, None),
            P("row", "col"),
            P("row", "col", None, None, None),
        ),
        out_specs=P(None, None, "row", "col"),
        check_vma=False,
    )
```
